32 devices in a mesh: groups: 2 (over y), seq: 4 (over z), head: 2 (over x), rep: 2 (over core).
Axes of the slice: x: 2, y: 2, z: 4, core: 2. Of those that a mesh axis runs over, the one named last changes fastest.
Arguments:
- queries: bfloat16 [8192, 5120], P(('groups', 'seq'), ('head', 'rep')), parts along dimension 0, may hold values from -4.5 to 4.5
- keys: bfloat16 [8192, 5120], P(('groups', 'seq'), ('head', 'rep')), parts along dimension 0, may hold values from -4.5 to 4.5
- values: bfloat16 [8192, 5120], P(('groups', 'seq'), ('head', 'rep')), parts along dimension 0, may hold values from -5 to 5
- rates: float32 [40, 8192], P(('head', 'rep'), ('groups', 'seq')), parts along dimension 1, may hold values from 0.0005 to 0.005
- fast_weights: bfloat16 [128, 40, 3, 128], P(None, ('head', 'rep')), may hold values from -0.5 to 0.5
- momentum: float32 [128, 40, 3, 128], P('seq', ('head', 'rep')), may hold values from -0.3 to 0.3
Outputs:
- mixed: bfloat16 [8192, 5120], P(('groups', 'seq'), ('head', 'rep')), parts along dimension 0
- new_weights: bfloat16 [256, 40, 3, 128], P(('groups', 'seq'), ('head', 'rep')), parts along dimension 0
- new_momentum: float32 [256, 40, 3, 128], P(('groups', 'seq'), ('head', 'rep')), parts along dimension 0
The draws below stay inside these ranges and needn't reach their ends.
There are 2 independent parts, one for each index of `groups`. The reference program is written for one: setup_inputs(seed, part) draws one part's arguments, and reference() takes and returns one part's arrays. A program takes and returns all parts, laid end to end along the dimension named above; an argument that names none is the same for every part. Nothing has to cross between parts.
All inputs are finite; a program needn't handle non-finite values.
Results may differ from the reference program's by a relative error of at most 0.013.
Values may be sent and summed in bfloat16 or wider, within the bound.
A program may use at most 128 MiB of HBM per device.

```python
import math
import jax
import jax.numpy as jnp
from jax import lax

HEADS = 40
DH = 128
FH = 128
WIN = 512
TOKENS = 4096


def query_key_pair(key):
    base = jax.random.fold_in(key, 7301)
    shape = (TOKENS, HEADS * DH)
    queries = jax.random.truncated_normal(jax.random.fold_in(base, 1), -4.0, 4.0, shape, jnp.float32)
    keys = jax.random.truncated_normal(jax.random.fold_in(base, 2), -4.0, 4.0, shape, jnp.float32)
    return (queries, keys)


def draw_queries(key, part):
    return query_key_pair(key)[0].astype(jnp.bfloat16)


def draw_keys(key, part):
    return query_key_pair(key)[1].astype(jnp.bfloat16)


def block_levels(key, dims, pieces, low, largest):
    level, own = 1.0, jax.random.fold_in(key, 6)
    for position, parts in pieces:
        heights = jnp.exp(jax.random.uniform(jax.random.fold_in(own, position), (parts,), jnp.float32, low / len(pieces), largest / len(pieces)))
        level = level * jnp.repeat(heights, dims[position] // parts).reshape([-1 if axis == position else 1 for axis in range(len(dims))])
    return level


def noise(key, dims, spread, bound, cuts=(), kind=jnp.bfloat16):
    loudness = block_levels(key, dims, cuts, -0.22, 0.18) if cuts else 1.0
    drawn = jax.random.normal(key, dims, jnp.float32) * spread * loudness
    return jnp.minimum(jnp.maximum(drawn, -bound), bound).astype(kind)


def setup_inputs(seed: int = 0, part: int = 0) -> dict:
    streams_of = jax.random.split(jax.random.key(seed), 7)
    part_keys = jax.random.split(jax.random.fold_in(streams_of[6], part), 7)
    return {
        "queries": draw_queries(jax.random.fold_in(jax.random.fold_in(streams_of[6], part), 71), part),
        "keys": draw_keys(jax.random.fold_in(jax.random.fold_in(streams_of[6], part), 71), part),
        "values": noise(part_keys[2], (TOKENS, HEADS * DH), 1.0, 5.0, ((0, 4), (1, 4))),
        "rates": jnp.clip(jnp.exp(math.log(0.005) - 2.30258502 * jax.random.uniform(part_keys[3], (HEADS, TOKENS), jnp.float32) ** block_levels(part_keys[3], (HEADS, TOKENS), ((0, 4), (1, 4)), -0.2, 0.2)), 0.0005, 0.005),
        "fast_weights": noise(streams_of[4], (DH, HEADS, 3, FH), DH ** -0.5, 0.5, ((1, 4),)),
        "momentum": noise(streams_of[5], (DH, HEADS, 3, FH), 0.05, 0.3, ((0, 4), (1, 4)), jnp.float32),
    }


momentum_keep = 0.9
epsilon = 1e-06

def window_block(query_block, key_block, value_block, first):
    width = query_block.shape[0]
    head_size = query_block.shape[2]
    scores = jnp.einsum('qhd,khd->hqk', query_block.astype(jnp.float32), key_block.astype(jnp.float32)) * head_size ** (-0.5)
    query_index = jnp.arange(width, dtype=jnp.int32)[:, None]
    key_index = jnp.arange(2 * width, dtype=jnp.int32)[None, :]
    allowed = (key_index > query_index) & (key_index <= query_index + width) & (key_index + first >= 0)
    scores = jnp.where(allowed[None], scores, -1e+30)
    row_max = lax.optimization_barrier(jnp.max(scores, axis=-1, keepdims=True))
    weights = jnp.exp(scores - row_max)
    total = lax.optimization_barrier(jnp.sum(weights, axis=-1, keepdims=True))
    probabilities = (weights / total).astype(jnp.bfloat16)
    return jnp.einsum('hqk,khd->qhd', probabilities.astype(jnp.float32), value_block.astype(jnp.float32))

def swiglu_parts(inputs, weights):
    inner = jnp.einsum('thr,rhcf->thcf', inputs.astype(jnp.float32), weights[:, :, 0:2].astype(jnp.float32))
    return (inner[:, :, 0], inner[:, :, 1])

def reference(queries, keys, values, rates, fast_weights, momentum):
    query_heads = queries.reshape(TOKENS, HEADS, DH)
    key_heads = keys.reshape(TOKENS, HEADS, DH)
    value_heads = values.reshape(TOKENS, HEADS, DH)
    gating, upward = swiglu_parts(key_heads, fast_weights)
    sigmoid_gate = jax.nn.sigmoid(gating)
    hidden = (gating * sigmoid_gate * upward).astype(jnp.bfloat16)
    scaled_values = (value_heads.astype(jnp.float32) * jnp.transpose(rates)[:, :, None]).astype(jnp.bfloat16)
    hidden_grad = jnp.einsum('thr,rhf->thf', scaled_values.astype(jnp.float32), fast_weights[:, :, 2].astype(jnp.float32))
    gate_grad = (hidden_grad * upward * sigmoid_gate * (1.0 + gating * (1.0 - sigmoid_gate))).astype(jnp.bfloat16)
    upward_grad = (hidden_grad * gating * sigmoid_gate).astype(jnp.bfloat16)
    paired = jnp.stack([gate_grad, upward_grad], axis=2)
    first_grads = jnp.einsum('thr,thcf->rhcf', key_heads.astype(jnp.float32), paired.astype(jnp.float32))
    second_grads = jnp.einsum('thr,thf->rhf', scaled_values.astype(jnp.float32), hidden.astype(jnp.float32))[:, :, None]
    grads = jnp.concatenate([first_grads, second_grads], axis=2)
    new_momentum = momentum_keep * momentum + grads
    before = fast_weights.astype(jnp.float32)
    moved = before + new_momentum
    ratio = jnp.sqrt((lax.optimization_barrier(jnp.mean(before * before, axis=-1, keepdims=True)) + epsilon) / (lax.optimization_barrier(jnp.mean(moved * moved, axis=-1, keepdims=True)) + epsilon))
    new_weights = (moved * ratio).astype(jnp.bfloat16)
    query_gating, query_upward = swiglu_parts(query_heads, new_weights)
    query_hidden = (jax.nn.silu(query_gating) * query_upward).astype(jnp.bfloat16)
    fast_out = jnp.einsum('thf,rhf->thr', query_hidden.astype(jnp.float32), new_weights[:, :, 2].astype(jnp.float32))
    padding = jnp.zeros((WIN, HEADS, DH), jnp.bfloat16)
    padded_keys = jnp.concatenate([padding, key_heads], axis=0)
    padded_values = jnp.concatenate([padding, value_heads], axis=0)

    def one_block(block):
        query_block = lax.dynamic_slice_in_dim(query_heads, block * WIN, WIN, 0)
        key_block = lax.dynamic_slice_in_dim(padded_keys, block * WIN, 2 * WIN, 0)
        value_block = lax.dynamic_slice_in_dim(padded_values, block * WIN, 2 * WIN, 0)
        return window_block(query_block, key_block, value_block, block * WIN - WIN)
    attended = lax.map(one_block, jnp.arange(TOKENS // WIN, dtype=jnp.int32)).reshape(TOKENS, HEADS, DH)
    mixed = (fast_out + attended).reshape(TOKENS, HEADS * DH).astype(jnp.bfloat16)
    return (mixed, new_weights, new_momentum)
```

```python
import functools
import math

import jax
import jax.numpy as jnp
from jax import lax
from jax.experimental import pallas as pl
from jax.experimental.pallas import tpu as pltpu
from jax.sharding import PartitionSpec as P

WIN = 512
momentum_keep = 0.9
epsilon = 1e-06
MESH = pl.DeviceIdType.MESH
F32 = jnp.float32
BF16 = jnp.bfloat16
NEG = -1e30
ROWS = WIN // 2


def dot_nn(a, b):
    return lax.dot_general(a, b, (((1,), (0,)), ((), ())), preferred_element_type=F32)


def dot_nt(a, b):
    return lax.dot_general(a, b, (((1,), (1,)), ((), ())), preferred_element_type=F32)


def dot_tn(a, b):
    return lax.dot_general(a, b, (((0,), (0,)), ((), ())), preferred_element_type=F32)


def kernel(
    n, heads, tok, d, own,
    q_hbm, k_hbm, v_hbm, r_ref, w_ref, wown_ref, mom_ref,
    out_hbm, nw_ref, nm_ref,
    qb, kb, vb, qr, att, lse, osend, orecv, stat, ssend, srecv, outb,
    gradb, gbuf, rsbuf, wnew,
    load_sem, out_sem, qs_sem, qr_sem, os_sem, or_sem, ss_sem, sr_sem,
    rs_s, rs_r, ag_s, ag_r,
):
    me = lax.axis_index("seq")
    first = me == 0
    last = me == n - 1
    scale = math.log2(math.e) / math.sqrt(d)
    before = lax.max(me - 1, 0)
    after = lax.min(me + 1, n - 1)

    def cols(h):
        return pl.ds(pl.multiple_of(h * d, d), d)

    def load(which, h):
        src = (q_hbm, k_hbm, v_hbm)[which]
        dst = (qb, kb, vb)[which]
        return pltpu.make_async_copy(src.at[:, cols(h)], dst.at[h], load_sem.at[which, h])

    def send_query(h):
        return pltpu.make_async_remote_copy(
            src_ref=q_hbm.at[pl.ds(0, WIN), cols(h)], dst_ref=qr.at[h],
            send_sem=qs_sem.at[h], recv_sem=qr_sem.at[h],
            device_id={"seq": before}, device_id_type=MESH)

    def send_result(h):
        return pltpu.make_async_remote_copy(
            src_ref=osend.at[h], dst_ref=orecv.at[h],
            send_sem=os_sem.at[h], recv_sem=or_sem.at[h],
            device_id={"seq": after}, device_id_type=MESH)

    def send_stats():
        return pltpu.make_async_remote_copy(
            src_ref=ssend, dst_ref=srecv, send_sem=ss_sem, recv_sem=sr_sem,
            device_id={"seq": after}, device_id_type=MESH)

    def send_grad(peer, h):
        return pltpu.make_async_remote_copy(
            src_ref=gbuf.at[peer, h], dst_ref=rsbuf.at[me, h],
            send_sem=rs_s.at[peer], recv_sem=rs_r.at[me],
            device_id={"seq": peer}, device_id_type=MESH)

    def whole_grad(peer):
        return pltpu.make_async_remote_copy(
            src_ref=gbuf.at[peer], dst_ref=rsbuf.at[peer],
            send_sem=rs_s.at[peer], recv_sem=rs_r.at[peer],
            device_id={"seq": peer}, device_id_type=MESH)

    def send_weights(peer, slot):
        return pltpu.make_async_remote_copy(
            src_ref=wnew.at[me], dst_ref=wnew.at[slot],
            send_sem=ag_s.at[peer], recv_sem=ag_r.at[slot],
            device_id={"seq": peer}, device_id_type=MESH)

    def each_peer(act):
        for step in range(1, n):
            act(lax.rem(me + step, n))

    def each_head(lo, hi, act):
        def body(h, carry):
            act(h)
            return carry
        lax.fori_loop(lo, hi, body, 0)

    def start_loads(h):
        load(1, h).start()
        load(2, h).start()

    each_head(0, heads, start_loads)
    barrier = pltpu.get_barrier_semaphore()
    each_peer(lambda peer: pl.semaphore_signal(
        barrier, inc=1, device_id={"seq": peer}, device_id_type=MESH))
    pl.semaphore_wait(barrier, n - 1)
    early = heads // 2

    @pl.when(jnp.logical_not(first))
    def _():
        each_head(0, early, lambda h: send_query(h).start())

    each_head(0, heads, lambda h: load(0, h).start())
    rows = lax.broadcasted_iota(jnp.int32, (ROWS, ROWS), 0)
    columns = lax.broadcasted_iota(jnp.int32, (ROWS, ROWS), 1)
    causal = columns <= rows
    ones = jnp.ones((ROWS, d), BF16)

    def gradient(h):
        load(1, h).wait()
        load(2, h).wait()
        weights = w_ref[h]
        lane = lax.broadcasted_iota(jnp.int32, (ROWS, heads), 1)
        total = jnp.zeros((d, 3 * d), F32)
        for b in range(tok // ROWS):
            part = slice(b * ROWS, (b + 1) * ROWS)
            keys = kb[h, part]
            rate = jnp.sum(jnp.where(lane == h, r_ref[part], 0.0), axis=1, keepdims=True)
            scaled = (vb[h, part].astype(F32) * rate).astype(BF16)
            inner = dot_nn(keys, weights[:, : 2 * d])
            gating, upward = inner[:, :d], inner[:, d:]
            sig = jax.nn.sigmoid(gating)
            silu = gating * sig
            hidden_grad = dot_nn(scaled, weights[:, 2 * d :])
            gradb[part, :d] = (hidden_grad * upward * sig * (1.0 + gating * (1.0 - sig))).astype(BF16)
            gradb[part, d : 2 * d] = (hidden_grad * silu).astype(BF16)
            gradb[part, 2 * d : 3 * d] = (silu * upward).astype(BF16)
            gradb[part, 3 * d :] = scaled
        one = dot_tn(kb[h], gradb[:, : 2 * d])
        two = dot_tn(gradb[:, 3 * d :], gradb[:, 2 * d : 3 * d])
        for p in range(n):
            part = slice(p * own, (p + 1) * own)
            gbuf[p, h, :, : 2 * d] = one[part].astype(BF16)
            gbuf[p, h, :, 2 * d :] = two[part].astype(BF16)
        each_peer(lambda peer: send_grad(peer, h).start())

    each_head(0, heads, gradient)

    @pl.when(jnp.logical_not(first))
    def _():
        each_head(early, heads, lambda h: send_query(h).start())

    def with_ones(values, blocks):
        return jnp.concatenate([values, jnp.concatenate([ones] * blocks, axis=0)], axis=1)

    def finish(acc, top):
        total = jnp.maximum(acc[:, d:], 1e-30)
        return acc[:, :d] / total, top * scale + jnp.log2(total)

    def edge(query, keys, values, keep, spare):
        blocks = keys.shape[0] // ROWS
        scores = dot_nt(query, keys)
        at = spare * ROWS
        masked = jnp.where(keep, scores[:, at : at + ROWS], NEG)
        top = masked
        if blocks == 2:
            full = scores[:, (1 - spare) * ROWS : (2 - spare) * ROWS]
            top = jnp.maximum(top, full)
        top = jnp.max(top, axis=1, keepdims=True)
        p = jnp.where(keep, jnp.exp2((masked - top) * scale), 0.0).astype(BF16)
        if blocks == 2:
            f = jnp.exp2((full - top) * scale).astype(BF16)
            p = jnp.concatenate([p, f] if spare == 0 else [f, p], axis=1)
        return finish(dot_nn(p, with_ones(values, blocks)), top)

    def inside(h, b):
        span = slice((b - 2) * ROWS, (b + 1) * ROWS)
        scores = dot_nt(qb[h, b * ROWS : (b + 1) * ROWS], kb[h, span])
        mixed = jnp.where(causal, scores[:, 2 * ROWS :], scores[:, :ROWS])
        full = scores[:, ROWS : 2 * ROWS]
        top = jnp.max(jnp.maximum(mixed, full), axis=1, keepdims=True)
        pm = jnp.exp2((mixed - top) * scale)
        pf = jnp.exp2((full - top) * scale).astype(BF16)
        p = jnp.concatenate(
            [jnp.where(causal, 0.0, pm).astype(BF16), pf, jnp.where(causal, pm, 0.0).astype(BF16)],
            axis=1)
        acc = dot_nn(p, with_ones(vb[h, span], 3))
        return acc[:, :d] / acc[:, d:]

    def local(h):
        load(0, h).wait()
        for b in range(tok // ROWS):
            part = slice(b * ROWS, (b + 1) * ROWS)
            if b < 2:
                span = slice(0, (b + 1) * ROWS)
                o, s = edge(qb[h, part], kb[h, span], vb[h, span], causal, b)
                lse[h, part] = s
            else:
                o = inside(h, b)
            att[h, part] = o

    each_head(0, heads, local)
    tail = tok - WIN

    def remote(h):
        send_query(h).wait_recv()
        lane = lax.broadcasted_iota(jnp.int32, (ROWS, 128), 1)
        for b in range(2):
            part = slice(b * ROWS, (b + 1) * ROWS)
            span = slice(tail + b * ROWS, tok)
            o, s = edge(qr[h, part], kb[h, span], vb[h, span], jnp.logical_not(causal), 0)
            osend[h, part] = o.astype(BF16)
            stat[part] = jnp.where(lane == h, s, stat[part])
        send_result(h).start()

    @pl.when(jnp.logical_not(last))
    def _():
        stat[...] = jnp.zeros_like(stat)
        each_head(0, early, remote)

    each_peer(lambda peer: whole_grad(peer).wait_recv())

    def refresh(h):
        total = gbuf[me, h].astype(F32)
        for step in range(1, n):
            total = total + rsbuf[lax.rem(me + step, n), h].astype(F32)
        moment = momentum_keep * mom_ref[h] + total
        nm_ref[h] = moment
        old = wown_ref[h].astype(F32)
        moved = old + moment
        for c in range(3):
            part = slice(c * d, (c + 1) * d)
            o, m = old[:, part], moved[:, part]
            ratio = jnp.sqrt(
                (jnp.mean(o * o, axis=1, keepdims=True) + epsilon)
                / (jnp.mean(m * m, axis=1, keepdims=True) + epsilon))
            new = (m * ratio).astype(BF16)
            wnew[me, h, :, part] = new
            nw_ref[h, :, part] = new

    each_head(0, heads, refresh)
    each_peer(lambda peer: send_weights(peer, me).start())

    @pl.when(jnp.logical_not(last))
    def _():
        each_head(early, heads, remote)
        ssend[...] = jnp.transpose(stat[...])[: ssend.shape[0]]
        send_stats().start()

    each_peer(lambda peer: send_weights(peer, peer).wait_recv())

    @pl.when(jnp.logical_not(first))
    def _():
        send_stats().wait_recv()
        held = srecv[...]
        stat2 = jnp.concatenate(
            [held, jnp.zeros((128 - held.shape[0], WIN), F32)], axis=0)
        stat[...] = jnp.transpose(stat2)

    def output(h):
        @pl.when(jnp.logical_not(first))
        def _():
            send_result(h).wait_recv()
            lane = lax.broadcasted_iota(jnp.int32, (ROWS, 128), 1)
            for b in range(2):
                part = slice(b * ROWS, (b + 1) * ROWS)
                theirs = jnp.sum(jnp.where(lane == h, stat[part], 0.0), axis=1, keepdims=True)
                ours = lse[h, part]
                top = jnp.maximum(ours, theirs)
                mine = jnp.exp2(ours - top)
                other = jnp.exp2(theirs - top)
                att[h, part] = (
                    att[h, part] * mine + orecv[h, part].astype(F32) * other) / (mine + other)

        weights = jnp.concatenate(
            [wnew[p, h].astype(F32) for p in range(n)], axis=0).astype(BF16)
        for b in range(tok // ROWS):
            part = slice(b * ROWS, (b + 1) * ROWS)
            inner = dot_nn(qb[h, part], weights[:, : 2 * d])
            gating, upward = inner[:, :d], inner[:, d:]
            hidden = (gating * jax.nn.sigmoid(gating) * upward).astype(BF16)
            fast = dot_nt(hidden, weights[:, 2 * d :])
            outb[h, part] = (fast + att[h, part]).astype(BF16)
        pltpu.make_async_copy(outb.at[h], out_hbm.at[:, cols(h)], out_sem.at[h]).start()

    each_head(0, heads, output)

    @pl.when(jnp.logical_not(first))
    def _():
        each_head(0, heads, lambda h: send_query(h).wait_send())

    @pl.when(jnp.logical_not(last))
    def _():
        each_head(0, heads, lambda h: send_result(h).wait_send())
        send_stats().wait_send()

    each_peer(lambda peer: whole_grad(peer).wait_send())
    each_peer(lambda peer: send_weights(peer, me).wait_send())
    each_head(0, heads, lambda h: pltpu.make_async_copy(
        outb.at[h], out_hbm.at[:, cols(h)], out_sem.at[h]).wait())


def shards(queries, keys, values, rates, fast_weights, momentum):
    n = lax.axis_size("seq")
    tok = queries.shape[0]
    heads = rates.shape[0]
    d = fast_weights.shape[0]
    own = momentum.shape[0]
    stat_rows = -(-heads // 8) * 8

    def by_head(x):
        return jnp.transpose(x, (1, 0, 2, 3)).reshape(heads, x.shape[0], 3 * d)

    mine = lax.dynamic_slice_in_dim(fast_weights, lax.axis_index("seq") * own, own, 0)
    vmem = pl.BlockSpec(memory_space=pltpu.VMEM)
    hbm = pl.BlockSpec(memory_space=pl.ANY)
    dma = pltpu.SemaphoreType.DMA
    out, weights, moments = pl.pallas_call(
        functools.partial(kernel, n, heads, tok, d, own),
        out_shape=(
            jax.ShapeDtypeStruct(queries.shape, BF16),
            jax.ShapeDtypeStruct((heads, own, 3 * d), BF16),
            jax.ShapeDtypeStruct((heads, own, 3 * d), F32),
        ),
        in_specs=[hbm, hbm, hbm, vmem, vmem, vmem, vmem],
        out_specs=(hbm, vmem, vmem),
        scratch_shapes=[
            pltpu.VMEM((heads, tok, d), BF16),
            pltpu.VMEM((heads, tok, d), BF16),
            pltpu.VMEM((heads, tok, d), BF16),
            pltpu.VMEM((heads, WIN, d), BF16),
            pltpu.VMEM((heads, tok, d), F32),
            pltpu.VMEM((heads, WIN, d), F32),
            pltpu.VMEM((heads, WIN, d), BF16),
            pltpu.VMEM((heads, WIN, d), BF16),
            pltpu.VMEM((WIN, 128), F32),
            pltpu.VMEM((stat_rows, WIN), F32),
            pltpu.VMEM((stat_rows, WIN), F32),
            pltpu.VMEM((heads, tok, d), BF16),
            pltpu.VMEM((tok, 4 * d), BF16),
            pltpu.VMEM((n, heads, own, 3 * d), BF16),
            pltpu.VMEM((n, heads, own, 3 * d), BF16),
            pltpu.VMEM((n, heads, own, 3 * d), BF16),
            dma((3, heads)), dma((heads,)), dma((heads,)), dma((heads,)),
            dma((heads,)), dma((heads,)), dma, dma,
            dma((n,)), dma((n,)), dma((n,)), dma((n,)),
        ],
        compiler_params=pltpu.CompilerParams(
            collective_id=0, has_side_effects=True, vmem_limit_bytes=60 * 1024 * 1024),
    )(queries, keys, values, jnp.transpose(rates), by_head(fast_weights), by_head(mine),
      by_head(momentum))

    def by_row(x):
        return jnp.transpose(x.reshape(heads, own, 3, d), (1, 0, 2, 3))

    return (out, by_row(weights), by_row(moments))


def solution(mesh):
    return jax.shard_map(
        shards,
        mesh=mesh,
        in_specs=(
            P(("groups", "seq"), ("head", "rep")),
            P(("groups", "seq"), ("head", "rep")),
            P(("groups", "seq"), ("head", "rep")),
            P(("head", "rep"), ("groups", "seq")),
            P(None, ("head", "rep"), None, None),
            P("seq", ("head", "rep"), None, None),
        ),
        out_specs=(
            P(("groups", "seq"), ("head", "rep")),
            P(("groups", "seq"), ("head", "rep"), None, None),
            P(("groups", "seq"), ("head", "rep"), None, None),
        ),
        check_vma=False,
    )
```

```python
import functools
import math

import jax
import jax.numpy as jnp
from jax import lax
from jax.experimental import pallas as pl
from jax.experimental.pallas import tpu as pltpu
from jax.sharding import PartitionSpec as P

WIN = 512
momentum_keep = 0.9
epsilon = 1e-06
MESH = pl.DeviceIdType.MESH
F32 = jnp.float32
BF16 = jnp.bfloat16
NEG = -1e30
ROWS = WIN // 2


def dot_nn(a, b):
    return lax.dot_general(a, b, (((1,), (0,)), ((), ())), preferred_element_type=F32)


def dot_nt(a, b):
    return lax.dot_general(a, b, (((1,), (1,)), ((), ())), preferred_element_type=F32)


def dot_tn(a, b):
    return lax.dot_general(a, b, (((0,), (0,)), ((), ())), preferred_element_type=F32)


def kernel(
    n, heads, tok, d, own,
    q_hbm, k_hbm, v_hbm, r_ref, w_hbm, mom_ref,
    out_hbm, nw_ref, nm_ref,
    rateb, wb, wown, qb, kb, vb, qr, att, lse, osend, orecv, stat, ssend, srecv, outb,
    gradb, gbuf, rsbuf, wnew,
    w_sem, load_sem, out_sem, qs_sem, qr_sem, os_sem, or_sem, ss_sem, sr_sem,
    rs_s, rs_r, ag_s, ag_r,
):
    me = lax.axis_index("seq")
    first = me == 0
    last = me == n - 1
    scale = math.log2(math.e) / math.sqrt(d)
    before = lax.max(me - 1, 0)
    after = lax.min(me + 1, n - 1)

    def cols(h):
        return pl.ds(pl.multiple_of(h * d, d), d)

    def load(which, h):
        src = (q_hbm, k_hbm, v_hbm)[which]
        dst = (qb, kb, vb)[which]
        return pltpu.make_async_copy(src.at[:, cols(h)], dst.at[h], load_sem.at[which, h])

    def send_query(h):
        return pltpu.make_async_remote_copy(
            src_ref=q_hbm.at[pl.ds(0, WIN), cols(h)], dst_ref=qr.at[h],
            send_sem=qs_sem.at[h], recv_sem=qr_sem.at[h],
            device_id={"seq": before}, device_id_type=MESH)

    def send_result(h):
        return pltpu.make_async_remote_copy(
            src_ref=osend.at[h], dst_ref=orecv.at[h],
            send_sem=os_sem.at[h], recv_sem=or_sem.at[h],
            device_id={"seq": after}, device_id_type=MESH)

    def send_stats():
        return pltpu.make_async_remote_copy(
            src_ref=ssend, dst_ref=srecv, send_sem=ss_sem, recv_sem=sr_sem,
            device_id={"seq": after}, device_id_type=MESH)

    def send_grad(j, step, h=None):
        peer = jnp.clip(me + step, 0, n - 1)
        slot = j if step == 1 else jnp.where(peer == j, n, j)
        src, dst = gbuf.at[j], rsbuf.at[slot]
        if h is not None:
            src, dst = gbuf.at[j, h], rsbuf.at[slot, h]
        return pltpu.make_async_remote_copy(
            src_ref=src, dst_ref=dst, send_sem=rs_s.at[j], recv_sem=rs_r.at[slot],
            device_id={"seq": peer}, device_id_type=MESH)

    def arrived(slot):
        pltpu.make_async_remote_copy(
            src_ref=gbuf.at[0], dst_ref=rsbuf.at[slot], send_sem=rs_s.at[0],
            recv_sem=rs_r.at[slot], device_id={"seq": before}, device_id_type=MESH).wait_recv()

    def send_weights(j, step):
        peer = before if step < 0 else after
        return pltpu.make_async_remote_copy(
            src_ref=wnew.at[j], dst_ref=wnew.at[j],
            send_sem=ag_s.at[0 if step < 0 else 1, j], recv_sem=ag_r.at[j],
            device_id={"seq": peer}, device_id_type=MESH)

    def relay(step):
        for j in range(n) if step < 0 else reversed(range(n)):
            @pl.when(j < me if step < 0 else j > me)
            def _():
                arrived(j)
                def add(h, carry):
                    gbuf[j, h] = (gbuf[j, h].astype(F32) + rsbuf[j, h].astype(F32)).astype(BF16)
                    return carry
                lax.fori_loop(0, heads, add, 0)
                send_grad(j, step).start()

    inner = jnp.logical_and(me > 0, me < n - 1)
    near = jnp.logical_and(inner, me < n // 2)
    far = jnp.logical_and(inner, me >= n // 2)

    def each_head(lo, hi, act):
        def body(h, carry):
            act(h)
            return carry
        lax.fori_loop(lo, hi, body, 0)

    def start_loads(h):
        load(1, h).start()
        load(2, h).start()

    own_rows = pl.ds(pl.multiple_of(me * own, own), own)
    load_weights = pltpu.make_async_copy(w_hbm, wb, w_sem.at[0])
    load_own = pltpu.make_async_copy(w_hbm.at[:, :, own_rows, :], wown, w_sem.at[1])
    load_weights.start()
    each_head(0, heads, start_loads)
    load_own.start()
    barrier = pltpu.get_barrier_semaphore()

    @pl.when(jnp.logical_not(first))
    def _():
        pl.semaphore_signal(barrier, inc=1, device_id={"seq": before}, device_id_type=MESH)

    @pl.when(jnp.logical_not(last))
    def _():
        pl.semaphore_signal(barrier, inc=1, device_id={"seq": after}, device_id_type=MESH)

    @pl.when(inner)
    def _():
        pl.semaphore_wait(barrier, 2)

    @pl.when(jnp.logical_not(inner))
    def _():
        pl.semaphore_wait(barrier, 1)

    early = heads // 2

    @pl.when(jnp.logical_not(first))
    def _():
        each_head(0, early, lambda h: send_query(h).start())

    each_head(0, heads, lambda h: load(0, h).start())
    rows = lax.broadcasted_iota(jnp.int32, (ROWS, ROWS), 0)
    columns = lax.broadcasted_iota(jnp.int32, (ROWS, ROWS), 1)
    causal = columns <= rows
    ones = jnp.ones((ROWS, d), BF16)

    def gradient(h):
        load(1, h).wait()
        load(2, h).wait()
        weights = jnp.concatenate([wb[h, c] for c in range(3)], axis=1)
        lane = lax.broadcasted_iota(jnp.int32, (ROWS, 128), 1)
        for b in range(tok // ROWS):
            part = slice(b * ROWS, (b + 1) * ROWS)
            keys = kb[h, part]
            rate = jnp.sum(jnp.where(lane == h, rateb[part], 0.0), axis=1, keepdims=True)
            scaled = (vb[h, part].astype(F32) * rate).astype(BF16)
            pair = dot_nn(keys, weights[:, : 2 * d])
            gating, upward = pair[:, :d], pair[:, d:]
            sig = jax.nn.sigmoid(gating)
            silu = gating * sig
            hidden_grad = dot_nn(scaled, weights[:, 2 * d :])
            gradb[part, :d] = (hidden_grad * upward * sig * (1.0 + gating * (1.0 - sig))).astype(BF16)
            gradb[part, d : 2 * d] = (hidden_grad * silu).astype(BF16)
            gradb[part, 2 * d : 3 * d] = (silu * upward).astype(BF16)
            gradb[part, 3 * d :] = scaled
        one = dot_tn(kb[h], gradb[:, : 2 * d])
        two = dot_tn(gradb[:, 3 * d :], gradb[:, 2 * d : 3 * d])
        for p in range(n):
            part = slice(p * own, (p + 1) * own)
            gbuf[p, h, 0] = one[part, :d].astype(BF16)
            gbuf[p, h, 1] = one[part, d:].astype(BF16)
            gbuf[p, h, 2] = two[part].astype(BF16)

        @pl.when(first)
        def _():
            for j in reversed(range(1, n)):
                send_grad(j, 1, h).start()

        @pl.when(last)
        def _():
            for j in range(n - 1):
                send_grad(j, -1, h).start()

    held_rates = jnp.concatenate(
        [r_ref[...], jnp.zeros((128 - heads, tok), F32)], axis=0)
    rateb[...] = jnp.transpose(held_rates)
    load_weights.wait()
    each_head(0, heads, gradient)

    @pl.when(jnp.logical_not(first))
    def _():
        each_head(early, heads, lambda h: send_query(h).start())

    def with_ones(values, blocks):
        return jnp.concatenate([values, jnp.concatenate([ones] * blocks, axis=0)], axis=1)

    def finish(acc, top):
        total = jnp.maximum(acc[:, d:], 1e-30)
        return acc[:, :d] / total, top * scale + jnp.log2(total)

    def edge(query, keys, values, keep, spare):
        blocks = keys.shape[0] // ROWS
        scores = dot_nt(query, keys)
        at = spare * ROWS
        masked = jnp.where(keep, scores[:, at : at + ROWS], NEG)
        top = masked
        if blocks == 2:
            full = scores[:, (1 - spare) * ROWS : (2 - spare) * ROWS]
            top = jnp.maximum(top, full)
        top = jnp.max(top, axis=1, keepdims=True)
        p = jnp.where(keep, jnp.exp2((masked - top) * scale), 0.0).astype(BF16)
        if blocks == 2:
            f = jnp.exp2((full - top) * scale).astype(BF16)
            p = jnp.concatenate([p, f] if spare == 0 else [f, p], axis=1)
        return finish(dot_nn(p, with_ones(values, blocks)), top)

    def inside(h, b):
        span = slice((b - 2) * ROWS, (b + 1) * ROWS)
        scores = dot_nt(qb[h, b * ROWS : (b + 1) * ROWS], kb[h, span])
        mixed = jnp.where(causal, scores[:, 2 * ROWS :], scores[:, :ROWS])
        full = scores[:, ROWS : 2 * ROWS]
        top = jnp.max(jnp.maximum(mixed, full), axis=1, keepdims=True)
        pm = jnp.exp2((mixed - top) * scale)
        pf = jnp.exp2((full - top) * scale).astype(BF16)
        p = jnp.concatenate(
            [jnp.where(causal, 0.0, pm).astype(BF16), pf, jnp.where(causal, pm, 0.0).astype(BF16)],
            axis=1)
        acc = dot_nn(p, with_ones(vb[h, span], 3))
        return acc[:, :d] / acc[:, d:]

    def local(h):
        load(0, h).wait()
        for b in range(tok // ROWS):
            part = slice(b * ROWS, (b + 1) * ROWS)
            if b < 2:
                span = slice(0, (b + 1) * ROWS)
                o, s = edge(qb[h, part], kb[h, span], vb[h, span], causal, b)
                lse[h, part] = s
            else:
                o = inside(h, b)
            att[h, part] = o

    each_head(0, early, local)

    @pl.when(near)
    def _():
        relay(1)

    @pl.when(far)
    def _():
        relay(-1)

    each_head(early, heads, local)

    @pl.when(near)
    def _():
        relay(-1)

    @pl.when(far)
    def _():
        relay(1)

    tail = tok - WIN

    def remote(h):
        send_query(h).wait_recv()
        lane = lax.broadcasted_iota(jnp.int32, (ROWS, 128), 1)
        for b in range(2):
            part = slice(b * ROWS, (b + 1) * ROWS)
            span = slice(tail + b * ROWS, tok)
            o, s = edge(qr[h, part], kb[h, span], vb[h, span], jnp.logical_not(causal), 0)
            osend[h, part] = o.astype(BF16)
            stat[part] = jnp.where(lane == h, s, stat[part])
        send_result(h).start()

    @pl.when(jnp.logical_not(last))
    def _():
        stat[...] = jnp.zeros_like(stat)
        each_head(0, early, remote)

    @pl.when(jnp.logical_not(first))
    def _():
        arrived(me)

    @pl.when(jnp.logical_not(last))
    def _():
        arrived(n)

    load_own.wait()

    def refresh(h):
        for c in range(3):
            total = gbuf[me, h, c].astype(F32)
            total = total + jnp.where(first, 0.0, rsbuf[me, h, c].astype(F32))
            total = total + jnp.where(last, 0.0, rsbuf[n, h, c].astype(F32))
            moment = momentum_keep * mom_ref[h, c] + total
            nm_ref[h, c] = moment
            o = wown[h, c].astype(F32)
            m = o + moment
            ratio = jnp.sqrt(
                (jnp.mean(o * o, axis=1, keepdims=True) + epsilon)
                / (jnp.mean(m * m, axis=1, keepdims=True) + epsilon))
            new = (m * ratio).astype(BF16)
            wnew[me, h, c] = new
            nw_ref[h, c] = new

    each_head(0, heads, refresh)

    @pl.when(jnp.logical_not(last))
    def _():
        send_weights(me, 1).start()

    @pl.when(jnp.logical_not(first))
    def _():
        send_weights(me, -1).start()

    @pl.when(jnp.logical_not(last))
    def _():
        each_head(early, heads, remote)
        ssend[...] = jnp.transpose(stat[...])[: ssend.shape[0]]
        send_stats().start()

    for step in range(1, n):
        @pl.when(me >= step)
        def _():
            send_weights(me - step, 1).wait_recv()

            @pl.when(jnp.logical_not(last))
            def _():
                send_weights(me - step, 1).start()

        @pl.when(me + step < n)
        def _():
            send_weights(me + step, -1).wait_recv()

            @pl.when(jnp.logical_not(first))
            def _():
                send_weights(me + step, -1).start()


    @pl.when(jnp.logical_not(first))
    def _():
        send_stats().wait_recv()
        held = srecv[...]
        stat2 = jnp.concatenate(
            [held, jnp.zeros((128 - held.shape[0], WIN), F32)], axis=0)
        stat[...] = jnp.transpose(stat2)

    def output(h):
        @pl.when(jnp.logical_not(first))
        def _():
            send_result(h).wait_recv()
            lane = lax.broadcasted_iota(jnp.int32, (ROWS, 128), 1)
            for b in range(2):
                part = slice(b * ROWS, (b + 1) * ROWS)
                theirs = jnp.sum(jnp.where(lane == h, stat[part], 0.0), axis=1, keepdims=True)
                ours = lse[h, part]
                top = jnp.maximum(ours, theirs)
                mine = jnp.exp2(ours - top)
                other = jnp.exp2(theirs - top)
                att[h, part] = (
                    att[h, part] * mine + orecv[h, part].astype(F32) * other) / (mine + other)

        weights = jnp.concatenate(
            [jnp.concatenate([wnew[p, h, c].astype(F32) for p in range(n)], axis=0)
             for c in range(3)], axis=1).astype(BF16)
        for b in range(tok // ROWS):
            part = slice(b * ROWS, (b + 1) * ROWS)
            pair = dot_nn(qb[h, part], weights[:, : 2 * d])
            gating, upward = pair[:, :d], pair[:, d:]
            hidden = (gating * jax.nn.sigmoid(gating) * upward).astype(BF16)
            fast = dot_nt(hidden, weights[:, 2 * d :])
            outb[h, part] = (fast + att[h, part]).astype(BF16)
        pltpu.make_async_copy(outb.at[h], out_hbm.at[:, cols(h)], out_sem.at[h]).start()

    each_head(0, heads, output)

    @pl.when(jnp.logical_not(first))
    def _():
        each_head(0, heads, lambda h: send_query(h).wait_send())

    @pl.when(jnp.logical_not(last))
    def _():
        each_head(0, heads, lambda h: send_result(h).wait_send())
        send_stats().wait_send()

    for j in range(n):
        @pl.when(j != me)
        def _():
            send_grad(j, 1).wait_send()

        @pl.when(jnp.logical_and(j <= me, me < n - 1))
        def _():
            send_weights(j, 1).wait_send()

        @pl.when(jnp.logical_and(j >= me, me > 0))
        def _():
            send_weights(j, -1).wait_send()

    each_head(0, heads, lambda h: pltpu.make_async_copy(
        outb.at[h], out_hbm.at[:, cols(h)], out_sem.at[h]).wait())


def shards(queries, keys, values, rates, fast_weights, momentum):
    n = lax.axis_size("seq")
    tok = queries.shape[0]
    heads = rates.shape[0]
    d = fast_weights.shape[0]
    own = momentum.shape[0]
    stat_rows = -(-heads // 8) * 8

    def by_head(x):
        return jnp.transpose(x, (1, 2, 0, 3))

    def by_row(x):
        return jnp.transpose(x, (2, 0, 1, 3))

    vmem = pl.BlockSpec(memory_space=pltpu.VMEM)
    hbm = pl.BlockSpec(memory_space=pl.ANY)
    dma = pltpu.SemaphoreType.DMA
    out, weights, moments = pl.pallas_call(
        functools.partial(kernel, n, heads, tok, d, own),
        out_shape=(
            jax.ShapeDtypeStruct(queries.shape, BF16),
            jax.ShapeDtypeStruct((heads, 3, own, d), BF16),
            jax.ShapeDtypeStruct((heads, 3, own, d), F32),
        ),
        in_specs=[hbm, hbm, hbm, vmem, hbm, vmem],
        out_specs=(hbm, vmem, vmem),
        scratch_shapes=[
            pltpu.VMEM((tok, 128), F32),
            pltpu.VMEM((heads, 3, d, d), BF16),
            pltpu.VMEM((heads, 3, own, d), BF16),
            pltpu.VMEM((heads, tok, d), BF16),
            pltpu.VMEM((heads, tok, d), BF16),
            pltpu.VMEM((heads, tok, d), BF16),
            pltpu.VMEM((heads, WIN, d), BF16),
            pltpu.VMEM((heads, tok, d), F32),
            pltpu.VMEM((heads, WIN, d), F32),
            pltpu.VMEM((heads, WIN, d), BF16),
            pltpu.VMEM((heads, WIN, d), BF16),
            pltpu.VMEM((WIN, 128), F32),
            pltpu.VMEM((stat_rows, WIN), F32),
            pltpu.VMEM((stat_rows, WIN), F32),
            pltpu.VMEM((heads, tok, d), BF16),
            pltpu.VMEM((tok, 4 * d), BF16),
            pltpu.VMEM((n, heads, 3, own, d), BF16),
            pltpu.VMEM((n + 1, heads, 3, own, d), BF16),
            pltpu.VMEM((n, heads, 3, own, d), BF16),
            dma((2,)), dma((3, heads)), dma((heads,)), dma((heads,)), dma((heads,)),
            dma((heads,)), dma((heads,)), dma, dma,
            dma((n,)), dma((n + 1,)), dma((2, n)), dma((n,)),
        ],
        compiler_params=pltpu.CompilerParams(
            collective_id=0, has_side_effects=True, vmem_limit_bytes=60 * 1024 * 1024),
    )(queries, keys, values, rates, by_head(fast_weights), by_head(momentum))

    return (out, by_row(weights), by_row(moments))


def solution(mesh):
    return jax.shard_map(
        shards,
        mesh=mesh,
        in_specs=(
            P(("groups", "seq"), ("head", "rep")),
            P(("groups", "seq"), ("head", "rep")),
            P(("groups", "seq"), ("head", "rep")),
            P(("head", "rep"), ("groups", "seq")),
            P(None, ("head", "rep"), None, None),
            P("seq", ("head", "rep"), None, None),
        ),
        out_specs=(
            P(("groups", "seq"), ("head", "rep")),
            P(("groups", "seq"), ("head", "rep"), None, None),
            P(("groups", "seq"), ("head", "rep"), None, None),
        ),
        check_vma=False,
    )
```

```python
import functools
import math

import jax
import jax.numpy as jnp
from jax import lax
from jax.experimental import pallas as pl
from jax.experimental.pallas import tpu as pltpu
from jax.sharding import PartitionSpec as P

WIN = 512
momentum_keep = 0.9
epsilon = 1e-06
MESH = pl.DeviceIdType.MESH
F32 = jnp.float32
BF16 = jnp.bfloat16
NEG = -1e30
ROWS = WIN // 2


def dot_nn(a, b):
    return lax.dot_general(a, b, (((1,), (0,)), ((), ())), preferred_element_type=F32)


def dot_nt(a, b):
    return lax.dot_general(a, b, (((1,), (1,)), ((), ())), preferred_element_type=F32)


def dot_tn(a, b):
    return lax.dot_general(a, b, (((0,), (0,)), ((), ())), preferred_element_type=F32)


def kernel(
    n, heads, tok, d, own,
    q_hbm, k_hbm, v_hbm, r_ref, w_hbm, mom_ref,
    out_hbm, nw_ref, nm_ref,
    rateb, wb, wown, qb, kb, vb, qr, att, lse, osend, orecv, stat, ssend, srecv, outb,
    gradb, gbuf, rsbuf, wnew,
    w_sem, load_sem, out_sem, qs_sem, qr_sem, os_sem, or_sem, ss_sem, sr_sem,
    rs_s, rs_r, ag_s, ag_r,
):
    me = lax.axis_index("seq")
    first = me == 0
    last = me == n - 1
    scale = math.log2(math.e) / math.sqrt(d)
    before = lax.max(me - 1, 0)
    after = lax.min(me + 1, n - 1)

    def cols(h):
        return pl.ds(pl.multiple_of(h * d, d), d)

    def load(which, h):
        src = (q_hbm, k_hbm, v_hbm)[which]
        dst = (qb, kb, vb)[which]
        return pltpu.make_async_copy(src.at[:, cols(h)], dst.at[h], load_sem.at[which, h])

    def send_query(h):
        return pltpu.make_async_remote_copy(
            src_ref=q_hbm.at[pl.ds(0, WIN), cols(h)], dst_ref=qr.at[h],
            send_sem=qs_sem.at[h], recv_sem=qr_sem.at[h],
            device_id={"seq": before}, device_id_type=MESH)

    def send_result(h):
        return pltpu.make_async_remote_copy(
            src_ref=osend.at[h], dst_ref=orecv.at[h],
            send_sem=os_sem.at[h], recv_sem=or_sem.at[h],
            device_id={"seq": after}, device_id_type=MESH)

    def send_stats():
        return pltpu.make_async_remote_copy(
            src_ref=ssend, dst_ref=srecv, send_sem=ss_sem, recv_sem=sr_sem,
            device_id={"seq": after}, device_id_type=MESH)

    def send_grad(j, step, h=None):
        peer = jnp.clip(me + step, 0, n - 1)
        slot = j if step == 1 else jnp.where(peer == j, n, j)
        src, dst = gbuf.at[j], rsbuf.at[slot]
        if h is not None:
            src, dst = gbuf.at[j, h], rsbuf.at[slot, h]
        return pltpu.make_async_remote_copy(
            src_ref=src, dst_ref=dst, send_sem=rs_s.at[j], recv_sem=rs_r.at[slot],
            device_id={"seq": peer}, device_id_type=MESH)

    def arrived(slot):
        pltpu.make_async_remote_copy(
            src_ref=gbuf.at[0], dst_ref=rsbuf.at[slot], send_sem=rs_s.at[0],
            recv_sem=rs_r.at[slot], device_id={"seq": before}, device_id_type=MESH).wait_recv()

    def send_weights(j, step):
        peer = before if step < 0 else after
        return pltpu.make_async_remote_copy(
            src_ref=wnew.at[j], dst_ref=wnew.at[j],
            send_sem=ag_s.at[0 if step < 0 else 1, j], recv_sem=ag_r.at[j],
            device_id={"seq": peer}, device_id_type=MESH)

    def relay(step):
        for j in range(n) if step < 0 else reversed(range(n)):
            @pl.when(j < me if step < 0 else j > me)
            def _():
                arrived(j)
                def add(h, carry):
                    gbuf[j, h] = (gbuf[j, h].astype(F32) + rsbuf[j, h].astype(F32)).astype(BF16)
                    return carry
                lax.fori_loop(0, heads, add, 0)
                send_grad(j, step).start()

    inner = jnp.logical_and(me > 0, me < n - 1)
    near = jnp.logical_and(inner, me < n // 2)
    far = jnp.logical_and(inner, me >= n // 2)

    def each_head(lo, hi, act):
        def body(h, carry):
            act(h)
            return carry
        lax.fori_loop(lo, hi, body, 0)

    def start_loads(h):
        load(1, h).start()
        load(2, h).start()

    own_rows = pl.ds(pl.multiple_of(me * own, own), own)
    load_weights = pltpu.make_async_copy(w_hbm, wb, w_sem.at[0])
    load_own = pltpu.make_async_copy(w_hbm.at[:, :, own_rows, :], wown, w_sem.at[1])
    load_weights.start()
    each_head(0, heads, start_loads)
    load_own.start()
    barrier = pltpu.get_barrier_semaphore()

    @pl.when(jnp.logical_not(first))
    def _():
        pl.semaphore_signal(barrier, inc=1, device_id={"seq": before}, device_id_type=MESH)

    @pl.when(jnp.logical_not(last))
    def _():
        pl.semaphore_signal(barrier, inc=1, device_id={"seq": after}, device_id_type=MESH)

    @pl.when(inner)
    def _():
        pl.semaphore_wait(barrier, 2)

    @pl.when(jnp.logical_not(inner))
    def _():
        pl.semaphore_wait(barrier, 1)

    early = heads * 7 // 10
    ahead = heads * 4 // 10
    left_half = me < n // 2
    r0 = jnp.where(last, 0, jnp.where(left_half, ahead, 0))
    r1 = jnp.where(last, 0, jnp.where(left_half, early, ahead))
    r2 = jnp.where(last, 0, early)
    r3 = jnp.where(last, 0, heads)

    @pl.when(inner)
    def _():
        each_head(0, early, lambda h: send_query(h).start())

    each_head(0, heads, lambda h: load(0, h).start())
    rows = lax.broadcasted_iota(jnp.int32, (ROWS, ROWS), 0)
    columns = lax.broadcasted_iota(jnp.int32, (ROWS, ROWS), 1)
    causal = columns <= rows
    ones = jnp.ones((ROWS, d), BF16)

    def gradient(h):
        load(1, h).wait()
        load(2, h).wait()
        weights = jnp.concatenate([wb[h, c] for c in range(3)], axis=1)
        lane = lax.broadcasted_iota(jnp.int32, (ROWS, 128), 1)
        for b in range(tok // ROWS):
            part = slice(b * ROWS, (b + 1) * ROWS)
            keys = kb[h, part]
            rate = jnp.sum(jnp.where(lane == h, rateb[part], 0.0), axis=1, keepdims=True)
            scaled = (vb[h, part].astype(F32) * rate).astype(BF16)
            pair = dot_nn(keys, weights[:, : 2 * d])
            gating, upward = pair[:, :d], pair[:, d:]
            sig = jax.nn.sigmoid(gating)
            silu = gating * sig
            hidden_grad = dot_nn(scaled, weights[:, 2 * d :])
            gradb[part, :d] = (hidden_grad * upward * sig * (1.0 + gating * (1.0 - sig))).astype(BF16)
            gradb[part, d : 2 * d] = (hidden_grad * silu).astype(BF16)
            gradb[part, 2 * d : 3 * d] = (silu * upward).astype(BF16)
            gradb[part, 3 * d :] = scaled
        one = dot_tn(kb[h], gradb[:, : 2 * d])
        two = dot_tn(gradb[:, 3 * d :], gradb[:, 2 * d : 3 * d])
        for p in range(n):
            part = slice(p * own, (p + 1) * own)
            gbuf[p, h, 0] = one[part, :d].astype(BF16)
            gbuf[p, h, 1] = one[part, d:].astype(BF16)
            gbuf[p, h, 2] = two[part].astype(BF16)

        @pl.when(first)
        def _():
            for j in reversed(range(1, n)):
                send_grad(j, 1, h).start()

        @pl.when(last)
        def _():
            for j in range(n - 1):
                send_grad(j, -1, h).start()

    held_rates = jnp.concatenate(
        [r_ref[...], jnp.zeros((128 - heads, tok), F32)], axis=0)
    rateb[...] = jnp.transpose(held_rates)
    load_weights.wait()
    each_head(0, heads, gradient)

    @pl.when(jnp.logical_and(last, jnp.logical_not(first)))
    def _():
        each_head(0, early, lambda h: send_query(h).start())

    def with_ones(values, blocks):
        return jnp.concatenate([values, jnp.concatenate([ones] * blocks, axis=0)], axis=1)

    def finish(acc, top):
        total = jnp.maximum(acc[:, d:], 1e-30)
        return acc[:, :d] / total, top * scale + jnp.log2(total)

    def edge(query, keys, values, keep, spare):
        blocks = keys.shape[0] // ROWS
        scores = dot_nt(query, keys)
        at = spare * ROWS
        masked = jnp.where(keep, scores[:, at : at + ROWS], NEG)
        top = masked
        if blocks == 2:
            full = scores[:, (1 - spare) * ROWS : (2 - spare) * ROWS]
            top = jnp.maximum(top, full)
        top = jnp.max(top, axis=1, keepdims=True)
        p = jnp.where(keep, jnp.exp2((masked - top) * scale), 0.0).astype(BF16)
        if blocks == 2:
            f = jnp.exp2((full - top) * scale).astype(BF16)
            p = jnp.concatenate([p, f] if spare == 0 else [f, p], axis=1)
        return finish(dot_nn(p, with_ones(values, blocks)), top)

    def inside(h, b):
        span = slice((b - 2) * ROWS, (b + 1) * ROWS)
        scores = dot_nt(qb[h, b * ROWS : (b + 1) * ROWS], kb[h, span])
        mixed = jnp.where(causal, scores[:, 2 * ROWS :], scores[:, :ROWS])
        full = scores[:, ROWS : 2 * ROWS]
        top = jnp.max(jnp.maximum(mixed, full), axis=1, keepdims=True)
        pm = jnp.exp2((mixed - top) * scale)
        pf = jnp.exp2((full - top) * scale).astype(BF16)
        p = jnp.concatenate(
            [jnp.where(causal, 0.0, pm).astype(BF16), pf, jnp.where(causal, pm, 0.0).astype(BF16)],
            axis=1)
        acc = dot_nn(p, with_ones(vb[h, span], 3))
        return acc[:, :d] / acc[:, d:]

    def local(h):
        load(0, h).wait()
        for b in range(tok // ROWS):
            part = slice(b * ROWS, (b + 1) * ROWS)
            if b < 2:
                span = slice(0, (b + 1) * ROWS)
                o, s = edge(qb[h, part], kb[h, span], vb[h, span], causal, b)
                lse[h, part] = s
            else:
                o = inside(h, b)
            att[h, part] = o

    tail = tok - WIN

    def remote(h):
        send_query(h).wait_recv()
        lane = lax.broadcasted_iota(jnp.int32, (ROWS, 128), 1)
        for b in range(2):
            part = slice(b * ROWS, (b + 1) * ROWS)
            span = slice(tail + b * ROWS, tok)
            o, s = edge(qr[h, part], kb[h, span], vb[h, span], jnp.logical_not(causal), 0)
            osend[h, part] = o.astype(BF16)
            stat[part] = jnp.where(lane == h, s, stat[part])
        send_result(h).start()

    stat[...] = jnp.zeros_like(stat)
    each_head(0, r0, remote)
    each_head(0, heads // 2, local)

    @pl.when(near)
    def _():
        relay(1)

    @pl.when(far)
    def _():
        relay(-1)

    each_head(heads // 2, heads, local)
    each_head(r0, r1, remote)

    @pl.when(near)
    def _():
        relay(-1)

    @pl.when(far)
    def _():
        relay(1)

    each_head(r1, r2, remote)

    @pl.when(jnp.logical_not(first))
    def _():
        arrived(me)

    @pl.when(jnp.logical_not(last))
    def _():
        arrived(n)

    load_own.wait()

    def refresh(h):
        for c in range(3):
            total = gbuf[me, h, c].astype(F32)
            total = total + jnp.where(first, 0.0, rsbuf[me, h, c].astype(F32))
            total = total + jnp.where(last, 0.0, rsbuf[n, h, c].astype(F32))
            moment = momentum_keep * mom_ref[h, c] + total
            nm_ref[h, c] = moment
            o = wown[h, c].astype(F32)
            m = o + moment
            ratio = jnp.sqrt(
                (jnp.mean(o * o, axis=1, keepdims=True) + epsilon)
                / (jnp.mean(m * m, axis=1, keepdims=True) + epsilon))
            new = (m * ratio).astype(BF16)
            wnew[me, h, c] = new
            nw_ref[h, c] = new

    each_head(0, heads, refresh)

    @pl.when(jnp.logical_not(last))
    def _():
        send_weights(me, 1).start()

    @pl.when(jnp.logical_not(first))
    def _():
        send_weights(me, -1).start()

    @pl.when(jnp.logical_not(first))
    def _():
        each_head(early, heads, lambda h: send_query(h).start())

    def pass_weights(step):
        @pl.when(me >= step)
        def _():
            send_weights(me - step, 1).wait_recv()

            @pl.when(jnp.logical_not(last))
            def _():
                send_weights(me - step, 1).start()

        @pl.when(me + step < n)
        def _():
            send_weights(me + step, -1).wait_recv()

            @pl.when(jnp.logical_not(first))
            def _():
                send_weights(me + step, -1).start()

    if n > 1:
        pass_weights(1)
    each_head(r2, r3, remote)

    @pl.when(jnp.logical_not(last))
    def _():
        ssend[...] = jnp.transpose(stat[...])[: ssend.shape[0]]
        send_stats().start()

    for step in range(2, n):
        pass_weights(step)

    @pl.when(jnp.logical_not(first))
    def _():
        send_stats().wait_recv()
        held = srecv[...]
        stat2 = jnp.concatenate(
            [held, jnp.zeros((128 - held.shape[0], WIN), F32)], axis=0)
        stat[...] = jnp.transpose(stat2)

    def output(h):
        @pl.when(jnp.logical_not(first))
        def _():
            send_result(h).wait_recv()
            lane = lax.broadcasted_iota(jnp.int32, (ROWS, 128), 1)
            for b in range(2):
                part = slice(b * ROWS, (b + 1) * ROWS)
                theirs = jnp.sum(jnp.where(lane == h, stat[part], 0.0), axis=1, keepdims=True)
                ours = lse[h, part]
                top = jnp.maximum(ours, theirs)
                mine = jnp.exp2(ours - top)
                other = jnp.exp2(theirs - top)
                att[h, part] = (
                    att[h, part] * mine + orecv[h, part].astype(F32) * other) / (mine + other)

        weights = jnp.concatenate(
            [jnp.concatenate([wnew[p, h, c].astype(F32) for p in range(n)], axis=0)
             for c in range(3)], axis=1).astype(BF16)
        for b in range(tok // ROWS):
            part = slice(b * ROWS, (b + 1) * ROWS)
            pair = dot_nn(qb[h, part], weights[:, : 2 * d])
            gating, upward = pair[:, :d], pair[:, d:]
            hidden = (gating * jax.nn.sigmoid(gating) * upward).astype(BF16)
            fast = dot_nt(hidden, weights[:, 2 * d :])
            outb[h, part] = (fast + att[h, part]).astype(BF16)
        pltpu.make_async_copy(outb.at[h], out_hbm.at[:, cols(h)], out_sem.at[h]).start()

    each_head(0, heads, output)

    @pl.when(jnp.logical_not(first))
    def _():
        each_head(0, heads, lambda h: send_query(h).wait_send())

    @pl.when(jnp.logical_not(last))
    def _():
        each_head(0, heads, lambda h: send_result(h).wait_send())
        send_stats().wait_send()

    for j in range(n):
        @pl.when(j != me)
        def _():
            send_grad(j, 1).wait_send()

        @pl.when(jnp.logical_and(j <= me, me < n - 1))
        def _():
            send_weights(j, 1).wait_send()

        @pl.when(jnp.logical_and(j >= me, me > 0))
        def _():
            send_weights(j, -1).wait_send()

    each_head(0, heads, lambda h: pltpu.make_async_copy(
        outb.at[h], out_hbm.at[:, cols(h)], out_sem.at[h]).wait())


def shards(queries, keys, values, rates, fast_weights, momentum):
    n = lax.axis_size("seq")
    tok = queries.shape[0]
    heads = rates.shape[0]
    d = fast_weights.shape[0]
    own = momentum.shape[0]
    stat_rows = -(-heads // 8) * 8

    def by_head(x):
        return jnp.transpose(x, (1, 2, 0, 3))

    def by_row(x):
        return jnp.transpose(x, (2, 0, 1, 3))

    vmem = pl.BlockSpec(memory_space=pltpu.VMEM)
    hbm = pl.BlockSpec(memory_space=pl.ANY)
    dma = pltpu.SemaphoreType.DMA
    out, weights, moments = pl.pallas_call(
        functools.partial(kernel, n, heads, tok, d, own),
        out_shape=(
            jax.ShapeDtypeStruct(queries.shape, BF16),
            jax.ShapeDtypeStruct((heads, 3, own, d), BF16),
            jax.ShapeDtypeStruct((heads, 3, own, d), F32),
        ),
        in_specs=[hbm, hbm, hbm, vmem, hbm, vmem],
        out_specs=(hbm, vmem, vmem),
        scratch_shapes=[
            pltpu.VMEM((tok, 128), F32),
            pltpu.VMEM((heads, 3, d, d), BF16),
            pltpu.VMEM((heads, 3, own, d), BF16),
            pltpu.VMEM((heads, tok, d), BF16),
            pltpu.VMEM((heads, tok, d), BF16),
            pltpu.VMEM((heads, tok, d), BF16),
            pltpu.VMEM((heads, WIN, d), BF16),
            pltpu.VMEM((heads, tok, d), F32),
            pltpu.VMEM((heads, WIN, d), F32),
            pltpu.VMEM((heads, WIN, d), BF16),
            pltpu.VMEM((heads, WIN, d), BF16),
            pltpu.VMEM((WIN, 128), F32),
            pltpu.VMEM((stat_rows, WIN), F32),
            pltpu.VMEM((stat_rows, WIN), F32),
            pltpu.VMEM((heads, tok, d), BF16),
            pltpu.VMEM((tok, 4 * d), BF16),
            pltpu.VMEM((n, heads, 3, own, d), BF16),
            pltpu.VMEM((n + 1, heads, 3, own, d), BF16),
            pltpu.VMEM((n, heads, 3, own, d), BF16),
            dma((2,)), dma((3, heads)), dma((heads,)), dma((heads,)), dma((heads,)),
            dma((heads,)), dma((heads,)), dma, dma,
            dma((n,)), dma((n + 1,)), dma((2, n)), dma((n,)),
        ],
        compiler_params=pltpu.CompilerParams(
            collective_id=0, has_side_effects=True, vmem_limit_bytes=60 * 1024 * 1024),
    )(queries, keys, values, rates, by_head(fast_weights), by_head(momentum))

    return (out, by_row(weights), by_row(moments))


def solution(mesh):
    return jax.shard_map(
        shards,
        mesh=mesh,
        in_specs=(
            P(("groups", "seq"), ("head", "rep")),
            P(("groups", "seq"), ("head", "rep")),
            P(("groups", "seq"), ("head", "rep")),
            P(("head", "rep"), ("groups", "seq")),
            P(None, ("head", "rep"), None, None),
            P("seq", ("head", "rep"), None, None),
        ),
        out_specs=(
            P(("groups", "seq"), ("head", "rep")),
            P(("groups", "seq"), ("head", "rep"), None, None),
            P(("groups", "seq"), ("head", "rep"), None, None),
        ),
        check_vma=False,
    )
```

```python
import functools
import math

import jax
import jax.numpy as jnp
from jax import lax
from jax.experimental import pallas as pl
from jax.experimental.pallas import tpu as pltpu
from jax.sharding import PartitionSpec as P

WIN = 512
momentum_keep = 0.9
epsilon = 1e-06
MESH = pl.DeviceIdType.MESH
F32 = jnp.float32
BF16 = jnp.bfloat16
NEG = -1e30
ROWS = WIN // 2


def dot_nn(a, b):
    return lax.dot_general(a, b, (((1,), (0,)), ((), ())), preferred_element_type=F32)


def dot_nt(a, b):
    return lax.dot_general(a, b, (((1,), (1,)), ((), ())), preferred_element_type=F32)


def dot_tn(a, b):
    return lax.dot_general(a, b, (((0,), (0,)), ((), ())), preferred_element_type=F32)


def kernel(
    n, heads, tok, d, own,
    q_hbm, k_hbm, v_hbm, r_ref, w_hbm, mom_ref,
    out_hbm, nw_ref, nm_ref,
    rateb, wb, wown, qb, kb, vb, qr, att, lse, osend, orecv, stat, ssend, srecv, outb,
    gradb, gbuf, rsbuf, wnew,
    w_sem, load_sem, out_sem, qs_sem, qr_sem, os_sem, or_sem, ss_sem, sr_sem,
    rs_s, rs_r, ag_s, ag_r,
):
    me = lax.axis_index("seq")
    first = me == 0
    last = me == n - 1
    scale = math.log2(math.e) / math.sqrt(d)
    before = lax.max(me - 1, 0)
    after = lax.min(me + 1, n - 1)

    def cols(h):
        return pl.ds(pl.multiple_of(h * d, d), d)

    def load(which, h):
        src = (q_hbm, k_hbm, v_hbm)[which]
        dst = (qb, kb, vb)[which]
        return pltpu.make_async_copy(src.at[:, cols(h)], dst.at[h], load_sem.at[which, h])

    def send_query(h):
        return pltpu.make_async_remote_copy(
            src_ref=q_hbm.at[pl.ds(0, WIN), cols(h)], dst_ref=qr.at[h],
            send_sem=qs_sem.at[h], recv_sem=qr_sem.at[h],
            device_id={"seq": before}, device_id_type=MESH)

    def send_result(h):
        return pltpu.make_async_remote_copy(
            src_ref=osend.at[h], dst_ref=orecv.at[h],
            send_sem=os_sem.at[h], recv_sem=or_sem.at[h],
            device_id={"seq": after}, device_id_type=MESH)

    def send_stats():
        return pltpu.make_async_remote_copy(
            src_ref=ssend, dst_ref=srecv, send_sem=ss_sem, recv_sem=sr_sem,
            device_id={"seq": after}, device_id_type=MESH)

    def send_grad(j, step, h=None):
        peer = jnp.clip(me + step, 0, n - 1)
        slot = j if step == 1 else jnp.where(peer == j, n, j)
        src, dst = gbuf.at[j], rsbuf.at[slot]
        if h is not None:
            src, dst = gbuf.at[j, h], rsbuf.at[slot, h]
        return pltpu.make_async_remote_copy(
            src_ref=src, dst_ref=dst, send_sem=rs_s.at[j], recv_sem=rs_r.at[slot],
            device_id={"seq": peer}, device_id_type=MESH)

    def arrived(slot):
        pltpu.make_async_remote_copy(
            src_ref=gbuf.at[0], dst_ref=rsbuf.at[slot], send_sem=rs_s.at[0],
            recv_sem=rs_r.at[slot], device_id={"seq": before}, device_id_type=MESH).wait_recv()

    def send_weights(j, step):
        peer = before if step < 0 else after
        return pltpu.make_async_remote_copy(
            src_ref=wnew.at[j], dst_ref=wnew.at[j],
            send_sem=ag_s.at[0 if step < 0 else 1, j], recv_sem=ag_r.at[j],
            device_id={"seq": peer}, device_id_type=MESH)

    def relay(step):
        for j in range(n) if step < 0 else reversed(range(n)):
            @pl.when(j < me if step < 0 else j > me)
            def _():
                arrived(j)
                def add(h, carry):
                    gbuf[j, h] = (gbuf[j, h].astype(F32) + rsbuf[j, h].astype(F32)).astype(BF16)
                    return carry
                lax.fori_loop(0, heads, add, 0)
                send_grad(j, step).start()

    inner = jnp.logical_and(me > 0, me < n - 1)
    near = jnp.logical_and(inner, me < n // 2)
    far = jnp.logical_and(inner, me >= n // 2)

    def each_head(lo, hi, act):
        def body(h, carry):
            act(h)
            return carry
        lax.fori_loop(lo, hi, body, 0)

    def start_loads(h):
        load(1, h).start()
        load(2, h).start()

    own_rows = pl.ds(pl.multiple_of(me * own, own), own)
    load_weights = pltpu.make_async_copy(w_hbm, wb, w_sem.at[0])
    load_own = pltpu.make_async_copy(w_hbm.at[:, :, own_rows, :], wown, w_sem.at[1])
    load_weights.start()
    each_head(0, heads, start_loads)
    load_own.start()
    barrier = pltpu.get_barrier_semaphore()

    @pl.when(jnp.logical_not(first))
    def _():
        pl.semaphore_signal(barrier, inc=1, device_id={"seq": before}, device_id_type=MESH)

    @pl.when(jnp.logical_not(last))
    def _():
        pl.semaphore_signal(barrier, inc=1, device_id={"seq": after}, device_id_type=MESH)

    @pl.when(inner)
    def _():
        pl.semaphore_wait(barrier, 2)

    @pl.when(jnp.logical_not(inner))
    def _():
        pl.semaphore_wait(barrier, 1)

    early = heads * 5 // 10
    ahead = heads * 3 // 10
    left_half = me < n // 2
    r0 = jnp.where(last, 0, jnp.where(left_half, ahead, 0))
    r1 = jnp.where(last, 0, jnp.where(left_half, early, ahead))
    r2 = jnp.where(last, 0, early)
    r3 = jnp.where(last, 0, heads)

    @pl.when(inner)
    def _():
        each_head(0, early, lambda h: send_query(h).start())

    each_head(0, heads, lambda h: load(0, h).start())
    rows = lax.broadcasted_iota(jnp.int32, (ROWS, ROWS), 0)
    columns = lax.broadcasted_iota(jnp.int32, (ROWS, ROWS), 1)
    causal = columns <= rows
    ones = jnp.ones((ROWS, d), BF16)

    def gradient(h):
        load(1, h).wait()
        load(2, h).wait()
        weights = jnp.concatenate([wb[h, c] for c in range(3)], axis=1)
        lane = lax.broadcasted_iota(jnp.int32, (ROWS, 128), 1)
        for b in range(tok // ROWS):
            part = slice(b * ROWS, (b + 1) * ROWS)
            keys = kb[h, part]
            rate = jnp.sum(jnp.where(lane == h, rateb[part], 0.0), axis=1, keepdims=True)
            scaled = (vb[h, part].astype(F32) * rate).astype(BF16)
            pair = dot_nn(keys, weights[:, : 2 * d])
            gating, upward = pair[:, :d], pair[:, d:]
            sig = jax.nn.sigmoid(gating)
            silu = gating * sig
            hidden_grad = dot_nn(scaled, weights[:, 2 * d :])
            gradb[part, :d] = (hidden_grad * upward * sig * (1.0 + gating * (1.0 - sig))).astype(BF16)
            gradb[part, d : 2 * d] = (hidden_grad * silu).astype(BF16)
            gradb[part, 2 * d : 3 * d] = (silu * upward).astype(BF16)
            gradb[part, 3 * d :] = scaled
        one = dot_tn(kb[h], gradb[:, : 2 * d])
        two = dot_tn(gradb[:, 3 * d :], gradb[:, 2 * d : 3 * d])
        for p in range(n):
            part = slice(p * own, (p + 1) * own)
            gbuf[p, h, 0] = one[part, :d].astype(BF16)
            gbuf[p, h, 1] = one[part, d:].astype(BF16)
            gbuf[p, h, 2] = two[part].astype(BF16)

        @pl.when(first)
        def _():
            for j in reversed(range(1, n)):
                send_grad(j, 1, h).start()

        @pl.when(last)
        def _():
            for j in range(n - 1):
                send_grad(j, -1, h).start()

    held_rates = jnp.concatenate(
        [r_ref[...], jnp.zeros((128 - heads, tok), F32)], axis=0)
    rateb[...] = jnp.transpose(held_rates)
    load_weights.wait()
    each_head(0, heads, gradient)

    @pl.when(jnp.logical_and(last, jnp.logical_not(first)))
    def _():
        each_head(0, early, lambda h: send_query(h).start())

    def with_ones(values, blocks):
        return jnp.concatenate([values, jnp.concatenate([ones] * blocks, axis=0)], axis=1)

    def finish(acc, top):
        total = jnp.maximum(acc[:, d:], 1e-30)
        return acc[:, :d] / total, top * scale + jnp.log2(total)

    def edge(query, keys, values, keep, spare):
        blocks = keys.shape[0] // ROWS
        scores = dot_nt(query, keys)
        at = spare * ROWS
        masked = jnp.where(keep, scores[:, at : at + ROWS], NEG)
        top = masked
        if blocks == 2:
            full = scores[:, (1 - spare) * ROWS : (2 - spare) * ROWS]
            top = jnp.maximum(top, full)
        top = jnp.max(top, axis=1, keepdims=True)
        p = jnp.where(keep, jnp.exp2((masked - top) * scale), 0.0).astype(BF16)
        if blocks == 2:
            f = jnp.exp2((full - top) * scale).astype(BF16)
            p = jnp.concatenate([p, f] if spare == 0 else [f, p], axis=1)
        return finish(dot_nn(p, with_ones(values, blocks)), top)

    def inside(h, b):
        span = slice((b - 2) * ROWS, (b + 1) * ROWS)
        scores = dot_nt(qb[h, b * ROWS : (b + 1) * ROWS], kb[h, span])
        mixed = jnp.where(causal, scores[:, 2 * ROWS :], scores[:, :ROWS])
        full = scores[:, ROWS : 2 * ROWS]
        top = jnp.max(jnp.maximum(mixed, full), axis=1, keepdims=True)
        pm = jnp.exp2((mixed - top) * scale)
        pf = jnp.exp2((full - top) * scale).astype(BF16)
        p = jnp.concatenate(
            [jnp.where(causal, 0.0, pm).astype(BF16), pf, jnp.where(causal, pm, 0.0).astype(BF16)],
            axis=1)
        acc = dot_nn(p, with_ones(vb[h, span], 3))
        return acc[:, :d] / acc[:, d:]

    def local(h):
        load(0, h).wait()
        for b in range(tok // ROWS):
            part = slice(b * ROWS, (b + 1) * ROWS)
            if b < 2:
                span = slice(0, (b + 1) * ROWS)
                o, s = edge(qb[h, part], kb[h, span], vb[h, span], causal, b)
                lse[h, part] = s
            else:
                o = inside(h, b)
            att[h, part] = o

    tail = tok - WIN

    def remote(h):
        send_query(h).wait_recv()
        lane = lax.broadcasted_iota(jnp.int32, (ROWS, 128), 1)
        for b in range(2):
            part = slice(b * ROWS, (b + 1) * ROWS)
            span = slice(tail + b * ROWS, tok)
            o, s = edge(qr[h, part], kb[h, span], vb[h, span], jnp.logical_not(causal), 0)
            osend[h, part] = o.astype(BF16)
            stat[part] = jnp.where(lane == h, s, stat[part])
        send_result(h).start()

    stat[...] = jnp.zeros_like(stat)
    each_head(0, r0, remote)
    each_head(0, heads // 2, local)

    @pl.when(near)
    def _():
        relay(1)

    @pl.when(far)
    def _():
        relay(-1)

    each_head(heads // 2, heads, local)
    each_head(r0, r1, remote)

    @pl.when(near)
    def _():
        relay(-1)

    @pl.when(far)
    def _():
        relay(1)

    each_head(r1, r2, remote)

    @pl.when(jnp.logical_not(first))
    def _():
        arrived(me)

    @pl.when(jnp.logical_not(last))
    def _():
        arrived(n)

    load_own.wait()

    def refresh(h):
        for c in range(3):
            total = gbuf[me, h, c].astype(F32)
            total = total + jnp.where(first, 0.0, rsbuf[me, h, c].astype(F32))
            total = total + jnp.where(last, 0.0, rsbuf[n, h, c].astype(F32))
            moment = momentum_keep * mom_ref[h, c] + total
            nm_ref[h, c] = moment
            o = wown[h, c].astype(F32)
            m = o + moment
            ratio = jnp.sqrt(
                (jnp.mean(o * o, axis=1, keepdims=True) + epsilon)
                / (jnp.mean(m * m, axis=1, keepdims=True) + epsilon))
            new = (m * ratio).astype(BF16)
            wnew[me, h, c] = new
            nw_ref[h, c] = new

    each_head(0, heads, refresh)

    @pl.when(jnp.logical_not(last))
    def _():
        send_weights(me, 1).start()

    @pl.when(jnp.logical_not(first))
    def _():
        send_weights(me, -1).start()

    @pl.when(jnp.logical_not(first))
    def _():
        each_head(early, heads, lambda h: send_query(h).start())

    def pass_weights(step):
        @pl.when(me >= step)
        def _():
            send_weights(me - step, 1).wait_recv()

            @pl.when(jnp.logical_not(last))
            def _():
                send_weights(me - step, 1).start()

        @pl.when(me + step < n)
        def _():
            send_weights(me + step, -1).wait_recv()

            @pl.when(jnp.logical_not(first))
            def _():
                send_weights(me + step, -1).start()

    if n > 1:
        pass_weights(1)
    each_head(r2, r3, remote)

    @pl.when(jnp.logical_not(last))
    def _():
        ssend[...] = jnp.transpose(stat[...])[: ssend.shape[0]]
        send_stats().start()

    for step in range(2, n):
        pass_weights(step)

    @pl.when(jnp.logical_not(first))
    def _():
        send_stats().wait_recv()
        held = srecv[...]
        stat2 = jnp.concatenate(
            [held, jnp.zeros((128 - held.shape[0], WIN), F32)], axis=0)
        stat[...] = jnp.transpose(stat2)

    def output(h):
        @pl.when(jnp.logical_not(first))
        def _():
            send_result(h).wait_recv()
            lane = lax.broadcasted_iota(jnp.int32, (ROWS, 128), 1)
            for b in range(2):
                part = slice(b * ROWS, (b + 1) * ROWS)
                theirs = jnp.sum(jnp.where(lane == h, stat[part], 0.0), axis=1, keepdims=True)
                ours = lse[h, part]
                top = jnp.maximum(ours, theirs)
                mine = jnp.exp2(ours - top)
                other = jnp.exp2(theirs - top)
                att[h, part] = (
                    att[h, part] * mine + orecv[h, part].astype(F32) * other) / (mine + other)

        weights = jnp.concatenate(
            [jnp.concatenate([wnew[p, h, c].astype(F32) for p in range(n)], axis=0)
             for c in range(3)], axis=1).astype(BF16)
        for b in range(tok // ROWS):
            part = slice(b * ROWS, (b + 1) * ROWS)
            pair = dot_nn(qb[h, part], weights[:, : 2 * d])
            gating, upward = pair[:, :d], pair[:, d:]
            hidden = (gating * jax.nn.sigmoid(gating) * upward).astype(BF16)
            fast = dot_nt(hidden, weights[:, 2 * d :])
            outb[h, part] = (fast + att[h, part]).astype(BF16)
        pltpu.make_async_copy(outb.at[h], out_hbm.at[:, cols(h)], out_sem.at[h]).start()

    each_head(0, heads, output)

    @pl.when(jnp.logical_not(first))
    def _():
        each_head(0, heads, lambda h: send_query(h).wait_send())

    @pl.when(jnp.logical_not(last))
    def _():
        each_head(0, heads, lambda h: send_result(h).wait_send())
        send_stats().wait_send()

    for j in range(n):
        @pl.when(j != me)
        def _():
            send_grad(j, 1).wait_send()

        @pl.when(jnp.logical_and(j <= me, me < n - 1))
        def _():
            send_weights(j, 1).wait_send()

        @pl.when(jnp.logical_and(j >= me, me > 0))
        def _():
            send_weights(j, -1).wait_send()

    each_head(0, heads, lambda h: pltpu.make_async_copy(
        outb.at[h], out_hbm.at[:, cols(h)], out_sem.at[h]).wait())


def shards(queries, keys, values, rates, fast_weights, momentum):
    n = lax.axis_size("seq")
    tok = queries.shape[0]
    heads = rates.shape[0]
    d = fast_weights.shape[0]
    own = momentum.shape[0]
    stat_rows = -(-heads // 8) * 8

    def by_head(x):
        return jnp.transpose(x, (1, 2, 0, 3))

    def by_row(x):
        return jnp.transpose(x, (2, 0, 1, 3))

    vmem = pl.BlockSpec(memory_space=pltpu.VMEM)
    hbm = pl.BlockSpec(memory_space=pl.ANY)
    dma = pltpu.SemaphoreType.DMA
    out, weights, moments = pl.pallas_call(
        functools.partial(kernel, n, heads, tok, d, own),
        out_shape=(
            jax.ShapeDtypeStruct(queries.shape, BF16),
            jax.ShapeDtypeStruct((heads, 3, own, d), BF16),
            jax.ShapeDtypeStruct((heads, 3, own, d), F32),
        ),
        in_specs=[hbm, hbm, hbm, vmem, hbm, vmem],
        out_specs=(hbm, vmem, vmem),
        scratch_shapes=[
            pltpu.VMEM((tok, 128), F32),
            pltpu.VMEM((heads, 3, d, d), BF16),
            pltpu.VMEM((heads, 3, own, d), BF16),
            pltpu.VMEM((heads, tok, d), BF16),
            pltpu.VMEM((heads, tok, d), BF16),
            pltpu.VMEM((heads, tok, d), BF16),
            pltpu.VMEM((heads, WIN, d), BF16),
            pltpu.VMEM((heads, tok, d), F32),
            pltpu.VMEM((heads, WIN, d), F32),
            pltpu.VMEM((heads, WIN, d), BF16),
            pltpu.VMEM((heads, WIN, d), BF16),
            pltpu.VMEM((WIN, 128), F32),
            pltpu.VMEM((stat_rows, WIN), F32),
            pltpu.VMEM((stat_rows, WIN), F32),
            pltpu.VMEM((heads, tok, d), BF16),
            pltpu.VMEM((tok, 4 * d), BF16),
            pltpu.VMEM((n, heads, 3, own, d), BF16),
            pltpu.VMEM((n + 1, heads, 3, own, d), BF16),
            pltpu.VMEM((n, heads, 3, own, d), BF16),
            dma((2,)), dma((3, heads)), dma((heads,)), dma((heads,)), dma((heads,)),
            dma((heads,)), dma((heads,)), dma, dma,
            dma((n,)), dma((n + 1,)), dma((2, n)), dma((n,)),
        ],
        compiler_params=pltpu.CompilerParams(
            collective_id=0, has_side_effects=True, vmem_limit_bytes=60 * 1024 * 1024),
    )(queries, keys, values, rates, by_head(fast_weights), by_head(momentum))

    return (out, by_row(weights), by_row(moments))


def solution(mesh):
    return jax.shard_map(
        shards,
        mesh=mesh,
        in_specs=(
            P(("groups", "seq"), ("head", "rep")),
            P(("groups", "seq"), ("head", "rep")),
            P(("groups", "seq"), ("head", "rep")),
            P(("head", "rep"), ("groups", "seq")),
            P(None, ("head", "rep"), None, None),
            P("seq", ("head", "rep"), None, None),
        ),
        out_specs=(
            P(("groups", "seq"), ("head", "rep")),
            P(("groups", "seq"), ("head", "rep"), None, None),
            P(("groups", "seq"), ("head", "rep"), None, None),
        ),
        check_vma=False,
    )
```
